512 devices in a mesh: leaf: 8 (over z), row: 4 (over x), col: 16 (over y, core).
Axes of the slice: x: 4, y: 8, z: 8, core: 2. Of those that a mesh axis runs over, the one named last changes fastest.
Arguments:
- leaf_rhs: float32 [16, 16, 4096], P('leaf', None, 'col'), may hold values from -6 to 6
- leaf_inverse: float32 [16, 4096, 4096], P('leaf', 'row', 'col'), as said below
- update_rows: float32 [16, 2048, 4096], P('leaf', 'col', 'row'), may hold values from -0.09375 to 0.09375
- update_map: int32 [16, 16], P('leaf'), may hold values from 0 to 31, as said below
- sep_rhs: float32 [16, 4096], replicated, may hold values from -6 to 6
- sep_inverse: float32 [4096, 4096], P(('leaf', 'row', 'col')), as said below
Outputs:
- leaf_solution: float32 [16, 16, 4096], P('leaf', None, ('col', 'row'))
- sep_solution: float32 [16, 4096], P(None, ('leaf', 'row', 'col'))
The draws below stay inside these ranges and needn't reach their ends.
Inputs may be any that keep to these rules, and one draw needn't show every extreme that they name: `update_map`: each row names 16 different separator blocks. `leaf_inverse`: entries off the diagonal are independent and of order 1 / sqrt(4096); each diagonal entry is one plus such a term. `sep_inverse`: entries off the diagonal are independent and of order 1 / sqrt(4096); each diagonal entry is one plus such a term.
All inputs are finite; a program needn't handle non-finite values.
Results may differ from the reference program's by a relative error of at most 0.000068.
Values sent between devices are 32-bit elements; how exact they have to be, the bound alone decides.
A program may use at most 64 MiB of HBM per device.

```python
import jax
import jax.numpy as jnp
from jax import lax

NL = 4096
NS = 4096
NRHS = 16
BLOCK = 128
NBLK = 16
SUBTREES = 16
NUP = 2048


def near_identity(key, count, order):
    noise = jax.random.normal(jax.random.fold_in(key, 11), (count, order, order), jnp.float32)
    return jnp.eye(order, dtype=jnp.float32)[None] + 0.7 * noise / jnp.sqrt(jnp.float32(order))


def draw_leaf_inverse(key, part):
    return near_identity(key, SUBTREES, NL)


def draw_sep_inverse(key, part):
    return near_identity(jax.random.fold_in(key, 5), 1, NS)[0]


def draw_update_map(key, part):
    keys = jax.random.split(jax.random.fold_in(key, 7), SUBTREES)
    picks = jax.vmap(lambda k: jax.random.permutation(k, NS // BLOCK)[:NBLK])(keys)
    return picks.astype(jnp.int32)


def block_levels(own_key, dims, cuts, low, largest):
    level = 1.0
    for position, shards_of in cuts:
        steps = jax.random.uniform(jax.random.fold_in(jax.random.fold_in(own_key, 6), position), (shards_of,), jnp.float32, low / len(cuts), largest / len(cuts))
        level = level * jnp.repeat(jnp.exp(steps), dims[position] // shards_of).reshape((-1,) + (1,) * (len(dims) - 1 - position))
    return level


def scatter_about(stream_key, dims, width, limit, shards=(), held_as=jnp.bfloat16):
    result = jax.random.normal(stream_key, dims, jnp.float32) * width
    if len(shards) > 0:
        result = block_levels(stream_key, dims, shards, -0.22, 0.18) * result
    return jnp.clip(result, min=-limit, max=limit).astype(held_as)


def setup_inputs(seed: int = 0) -> dict:
    splits = jax.random.split(jax.random.key(seed), 7)
    leaf_rhs = scatter_about(splits[0], (SUBTREES, NRHS, NL), 1.0, 6.0, ((0, 8), (2, 16)), jnp.float32)
    leaf_inverse = draw_leaf_inverse(jax.random.fold_in(splits[6], 71), 0)
    update_rows = scatter_about(splits[2], (SUBTREES, NUP, NL), NL ** -0.5, 0.09375, ((0, 8), (1, 16), (2, 4)), jnp.float32)
    update_map = draw_update_map(jax.random.fold_in(splits[6], 71), 0)
    sep_rhs = scatter_about(splits[4], (NRHS, NS), 1.0, 6.0, (), jnp.float32)
    sep_inverse = draw_sep_inverse(jax.random.fold_in(splits[6], 71), 0)
    return dict(leaf_rhs=leaf_rhs, leaf_inverse=leaf_inverse, update_rows=update_rows, update_map=update_map, sep_rhs=sep_rhs, sep_inverse=sep_inverse)


HIGH = lax.Precision.HIGHEST


def reference(leaf_rhs, leaf_inverse, update_rows, update_map, sep_rhs, sep_inverse):
    nsb = NS // BLOCK
    subs = leaf_rhs.shape[0]
    forward = jnp.einsum('sij,srj->sri', leaf_inverse, leaf_rhs, precision=HIGH)
    coupled = jnp.einsum('sun,srn->sru', update_rows, forward, precision=HIGH)
    onehot = (update_map[:, :, None] == jnp.arange(nsb, dtype=jnp.int32)[None, None, :]).astype(jnp.float32)
    blocks = coupled.reshape(subs, NRHS, NBLK, BLOCK)
    scattered = jnp.einsum('srkc,skb->rbc', blocks, onehot, precision=HIGH).reshape(NRHS, NS)
    sep_forward = jnp.einsum('ij,rj->ri', sep_inverse, sep_rhs - scattered, precision=HIGH)
    sep_solution = jnp.einsum('ij,ri->rj', sep_inverse, sep_forward, precision=HIGH)
    pulled = jnp.einsum('rbc,skb->srkc', sep_solution.reshape(NRHS, nsb, BLOCK), onehot, precision=HIGH)
    pulled = pulled.reshape(subs, NRHS, NBLK * BLOCK)
    reduced = forward - jnp.einsum('sun,sru->srn', update_rows, pulled, precision=HIGH)
    leaf_solution = jnp.einsum('sij,sri->srj', leaf_inverse, reduced, precision=HIGH)
    return leaf_solution, sep_solution
```

```python
import functools

import jax
import jax.numpy as jnp
from jax import lax
from jax.experimental import pallas as pl
from jax.experimental.pallas import tpu as pltpu
from jax.sharding import PartitionSpec as P

BLOCK = 128
NZ, NX, NC, NY = 8, 4, 16, 8
F32 = jnp.float32
BF16 = jnp.bfloat16
NT = (((1,), (1,)), ((), ()))
NN = (((1,), (0,)), ((), ()))

COL_STEPS = [(dy, dc) for dy in (4, 3, 5, 2, 6, 1, 7, 0) for dc in (0, 1) if (dy, dc) != (0, 0)]
Z_STEPS = (4, 3, 5, 2, 6, 1, 7)
X_STEPS = (2, 1, 3)


def halves(a):
    hi = a.astype(BF16)
    return hi, (a - hi.astype(F32)).astype(BF16)


def dot3(a, b_hi, b_lo, dims):
    m = a.shape[0]
    a_hi, a_lo = halves(a)
    both = lax.dot_general(jnp.concatenate([a_hi, a_lo], axis=0), b_hi, dims, preferred_element_type=F32)
    rest = lax.dot_general(a_hi, b_lo, dims, preferred_element_type=F32)
    return both[:m] + (both[m:] + rest)


def kernel(
    map_ref, rhs_hbm, l_hbm, u_hbm, srhs_hbm, s_hbm, leaf_out, sep_out,
    rhs_v, l_v, u_v, srhs_v, l_hi, l_lo, u_hi, u_lo, s_v, s_hi, s_lo,
    part, a_rs, fwd, xs, b1, b2, b3s, b3, c_ar, d_ar, e1, e2s, e2, fs, f_rs, red, gs, g_rs,
    load_sem, send_sem, recv_sem,
):
    z = lax.axis_index("leaf")
    x = lax.axis_index("row")
    me = lax.axis_index("col")
    y = me // 2
    core = me % 2

    def col_peer(step):
        return lax.rem(y + step[0], NY) * 2 + lax.rem(core + step[1], 2)

    def z_peer(step):
        return lax.rem(z + step, NZ)

    def x_peer(step):
        return lax.rem(x + step, NX)

    barrier = pltpu.get_barrier_semaphore()
    for step in COL_STEPS:
        pl.semaphore_signal(barrier, inc=1, device_id={"col": col_peer(step)}, device_id_type=pl.DeviceIdType.MESH)
    for step in Z_STEPS:
        pl.semaphore_signal(barrier, inc=1, device_id={"leaf": z_peer(step)}, device_id_type=pl.DeviceIdType.MESH)
    for step in X_STEPS:
        pl.semaphore_signal(barrier, inc=1, device_id={"row": x_peer(step)}, device_id_type=pl.DeviceIdType.MESH)

    loads = [
        pltpu.make_async_copy(rhs_hbm, rhs_v, load_sem.at[0]),
        pltpu.make_async_copy(l_hbm.at[0], l_v.at[0], load_sem.at[1]),
        pltpu.make_async_copy(l_hbm.at[1], l_v.at[1], load_sem.at[2]),
        pltpu.make_async_copy(u_hbm, u_v, load_sem.at[3]),
        pltpu.make_async_copy(s_hbm.at[:, pl.ds(pl.multiple_of(z * 512, 512), 512)], s_v.at[x, z], load_sem.at[4]),
        pltpu.make_async_copy(srhs_hbm.at[:, pl.ds(pl.multiple_of(z * 512, 512), 512)], srhs_v, load_sem.at[5]),
    ]
    for copy in loads:
        copy.start()

    def send(stage, src, dst, where):
        pltpu.make_async_remote_copy(
            src_ref=src, dst_ref=dst, send_sem=send_sem.at[stage], recv_sem=recv_sem.at[stage],
            device_id=where, device_id_type=pl.DeviceIdType.MESH,
        ).start()

    def landed(stage, buf, count):
        view = buf.at[pl.ds(0, count)]
        pltpu.make_async_copy(view, view, recv_sem.at[stage]).wait()

    def drained(stage, buf, count):
        view = buf.at[pl.ds(0, count)]
        pltpu.make_async_copy(view, view, send_sem.at[stage]).wait()

    loads[0].wait()
    for s in range(2):
        loads[1 + s].wait()
        hi, lo = halves(l_v[s])
        l_hi[s] = hi
        l_lo[s] = lo
        p = dot3(rhs_v[s], hi, lo, NT)
        for j in range(8):
            part[s * 8 + j] = p[:, j * 128:(j + 1) * 128]

    pl.semaphore_wait(barrier, len(COL_STEPS) + len(Z_STEPS) + len(X_STEPS))
    for step in COL_STEPS:
        peer = col_peer(step)
        send(0, part.at[peer], a_rs.at[me], {"col": peer})
    for step in Z_STEPS:
        peer = z_peer(step)
        send(1, s_hbm.at[:, pl.ds(pl.multiple_of(peer * 512, 512), 512)], s_v.at[x, z], {"leaf": peer})
    a_rs[me] = part[me]
    loads[3].wait()
    for s in range(2):
        hi, lo = halves(u_v[s])
        u_hi[s] = hi
        u_lo[s] = lo
    landed(0, a_rs, 15)
    fwd[me] = jnp.sum(a_rs[...], axis=0)
    for step in COL_STEPS:
        peer = col_peer(step)
        send(2, fwd.at[me], fwd.at[me], {"col": peer})

    loads[4].wait()
    view = s_v.at[0, pl.ds(0, 7)]
    pltpu.make_async_copy(view, view, recv_sem.at[1]).wait()
    for step in X_STEPS:
        send(3, s_v.at[x], s_v.at[x], {"row": x_peer(step)})

    loads[5].wait()
    srhs4 = jnp.zeros((4, 512), F32)
    for k in range(NX):
        srhs4 = srhs4 + jnp.where(x == k, srhs_v[4 * k:4 * k + 4, :], 0.0)
    low = lax.broadcasted_iota(jnp.int32, (8, 128), 0) < 4

    landed(2, fwd, 15)
    coupled = []
    for s in range(2):
        f = jnp.concatenate([fwd[s * 8 + j] for j in range(8)], axis=1)
        coupled.append(dot3(f, u_hi[s], u_lo[s], NT))
    for k in range(NX):
        xs[k] = jnp.concatenate([coupled[0][4 * k:4 * k + 4], coupled[1][4 * k:4 * k + 4]], axis=0)
    for step in X_STEPS:
        peer = x_peer(step)
        send(4, xs.at[peer], b1.at[x], {"row": peer})
    b1[x] = xs[x]
    landed(4, b1, 3)
    b2[me] = jnp.sum(b1[...], axis=0)
    for step in COL_STEPS:
        send(5, b2.at[me], b2.at[me], {"col": col_peer(step)})

    landed(3, s_v, 3)
    for k in range(NX):
        hi, lo = halves(s_v[k].reshape(64, 512))
        s_hi[k * 64:(k + 1) * 64] = hi
        s_lo[k * 64:(k + 1) * 64] = lo
    which = [jnp.where(low, map_ref[0, k], map_ref[1, k]) for k in range(NC)]

    landed(5, b2, 15)
    tiles = [b2[k] for k in range(NC)]
    for b in range(0, 32, 2):
        pair = []
        for block in (b, b + 1):
            acc = jnp.where(which[0] == block, tiles[0], 0.0)
            for k in range(1, NC):
                acc = acc + jnp.where(which[k] == block, tiles[k], 0.0)
            pair.append(acc + pltpu.roll(acc, 4, 0))
        b3s[b // 4, (b // 2) % 2] = jnp.where(low, pair[0], pair[1])
    for step in Z_STEPS:
        peer = z_peer(step)
        send(6, b3s.at[peer], b3.at[z], {"leaf": peer})
    b3[z] = b3s[z]
    landed(6, b3, 7)
    scattered = jnp.sum(b3[...], axis=0)
    updated = srhs4 - jnp.concatenate(
        [scattered[0, 0:4], scattered[0, 4:8], scattered[1, 0:4], scattered[1, 4:8]], axis=1
    )
    sf = dot3(updated, s_hi[...], s_lo[...], NT)
    c_ar[z] = jnp.concatenate([sf[:, :128], sf[:, 128:]], axis=0)
    for step in Z_STEPS:
        send(7, c_ar.at[z], c_ar.at[z], {"leaf": z_peer(step)})
    landed(7, c_ar, 7)
    sf = jnp.sum(c_ar[...], axis=0)
    sf = jnp.concatenate([sf[0:4], sf[4:8]], axis=1)
    back = dot3(sf, s_hi[...], s_lo[...], NN)
    for p in range(2):
        d_ar[me, p] = jnp.concatenate(
            [back[:, p * 256:p * 256 + 128], back[:, p * 256 + 128:p * 256 + 256]], axis=0
        )
    for step in COL_STEPS:
        send(8, d_ar.at[me], d_ar.at[me], {"col": col_peer(step)})
    landed(8, d_ar, 15)
    sol = jnp.sum(d_ar[...], axis=0)
    e1[z] = sol
    for step in Z_STEPS:
        send(9, e1.at[z], e1.at[z], {"leaf": z_peer(step)})
    for k in range(NX):
        half = sol[k // 2, 4 * (k % 2):4 * (k % 2) + 4]
        e2s[k, 1] = jnp.concatenate([half, half], axis=0)
    landed(9, e1, 7)
    picked = []
    for s in range(2):
        target = map_ref[s, me]
        acc = jnp.zeros((8, 128), F32)
        for q in range(16):
            block = jnp.where(low, 2 * q, 2 * q + 1)
            acc = acc + jnp.where(block == target, e1[q // 2, q % 2], 0.0)
        picked.append(acc + pltpu.roll(acc, 4, 0))
    pulled_tile = jnp.where(low, picked[0], picked[1])
    for k in range(NX):
        e2s[k, 0] = pulled_tile
    for step in X_STEPS:
        peer = x_peer(step)
        send(10, e2s.at[peer], e2.at[x], {"row": peer})
    e2[x] = e2s[x]
    landed(10, e2, 3)
    for s in range(2):
        pulled = jnp.concatenate([e2[k, 0, 4 * s:4 * s + 4] for k in range(NX)], axis=0)
        p = dot3(pulled, u_hi[s], u_lo[s], NN)
        for j in range(8):
            fs[s * 8 + j] = p[:, j * 128:(j + 1) * 128]
    for step in COL_STEPS:
        peer = col_peer(step)
        send(11, fs.at[peer], f_rs.at[me], {"col": peer})
    f_rs[me] = fs[me]
    block = jnp.concatenate([e2[k, 1, 0:4] for k in range(NX)], axis=0)
    sep_out[...] = pltpu.roll(block, lax.rem(128 - 8 * me, 128), 1)[:, :8]
    landed(11, f_rs, 15)
    red[me] = fwd[me] - jnp.sum(f_rs[...], axis=0)
    for step in COL_STEPS:
        send(12, red.at[me], red.at[me], {"col": col_peer(step)})
    landed(12, red, 15)
    lp = []
    for s in range(2):
        f = jnp.concatenate([red[s * 8 + j] for j in range(8)], axis=1)
        lp.append(dot3(f, l_hi[s], l_lo[s], NN))
    for k in range(NX):
        gs[k] = jnp.concatenate([lp[0][:, k * 64:(k + 1) * 64], lp[1][:, k * 64:(k + 1) * 64]], axis=1)
    for step in X_STEPS:
        peer = x_peer(step)
        send(13, gs.at[peer], g_rs.at[x], {"row": peer})
    g_rs[x] = gs[x]
    drained(0, part, 15)
    view = s_v.at[0, pl.ds(0, 7)]
    pltpu.make_async_copy(view, view, send_sem.at[1]).wait()
    drained(2, fwd, 15)
    drained(3, s_v, 3)
    drained(4, xs, 3)
    drained(5, b2, 15)
    drained(6, b3s, 7)
    drained(7, c_ar, 7)
    drained(8, d_ar, 15)
    drained(9, e1, 7)
    drained(10, e2s, 3)
    drained(11, fs, 15)
    drained(12, red, 15)
    landed(13, g_rs, 3)
    total = jnp.sum(g_rs[...], axis=0)
    leaf_out[0] = total[:, :64]
    leaf_out[1] = total[:, 64:]
    drained(13, gs, 3)


def body(leaf_rhs, leaf_inverse, update_rows, update_map, sep_rhs, sep_inverse):
    hbm = pl.BlockSpec(memory_space=pl.ANY)
    vmem = pl.BlockSpec(memory_space=pltpu.VMEM)
    stages = 14
    return pl.pallas_call(
        kernel,
        name="substitution",
        out_shape=(jax.ShapeDtypeStruct((2, 16, 64), F32), jax.ShapeDtypeStruct((16, 8), F32)),
        in_specs=[pl.BlockSpec(memory_space=pltpu.SMEM), hbm, hbm, hbm, hbm, hbm],
        out_specs=(vmem, vmem),
        scratch_shapes=[
            pltpu.VMEM((2, 16, 256), F32),
            pltpu.VMEM((2, 1024, 256), F32),
            pltpu.VMEM((2, 128, 1024), F32),
            pltpu.VMEM((16, 512), F32),
            pltpu.VMEM((2, 1024, 256), BF16),
            pltpu.VMEM((2, 1024, 256), BF16),
            pltpu.VMEM((2, 128, 1024), BF16),
            pltpu.VMEM((2, 128, 1024), BF16),
            pltpu.VMEM((NX, NZ, 8, 512), F32),
            pltpu.VMEM((256, 512), BF16),
            pltpu.VMEM((256, 512), BF16),
            pltpu.VMEM((NC, 16, 128), F32),
            pltpu.VMEM((NC, 16, 128), F32),
            pltpu.VMEM((NC, 16, 128), F32),
            pltpu.VMEM((NX, 8, 128), F32),
            pltpu.VMEM((NX, 8, 128), F32),
            pltpu.VMEM((NC, 8, 128), F32),
            pltpu.VMEM((NZ, 2, 8, 128), F32),
            pltpu.VMEM((NZ, 2, 8, 128), F32),
            pltpu.VMEM((NZ, 8, 128), F32),
            pltpu.VMEM((NC, 2, 8, 128), F32),
            pltpu.VMEM((NZ, 2, 8, 128), F32),
            pltpu.VMEM((NX, 2, 8, 128), F32),
            pltpu.VMEM((NX, 2, 8, 128), F32),
            pltpu.VMEM((NC, 16, 128), F32),
            pltpu.VMEM((NC, 16, 128), F32),
            pltpu.VMEM((NC, 16, 128), F32),
            pltpu.VMEM((NX, 16, 128), F32),
            pltpu.VMEM((NX, 16, 128), F32),
            pltpu.SemaphoreType.DMA((6,)),
            pltpu.SemaphoreType.DMA((stages,)),
            pltpu.SemaphoreType.DMA((stages,)),
        ],
        compiler_params=pltpu.CompilerParams(collective_id=0, has_side_effects=True),
    )(update_map, leaf_rhs, leaf_inverse, update_rows, sep_rhs, sep_inverse)


def solution(mesh):
    in_specs = (
        P("leaf", None, "col"),
        P("leaf", "row", "col"),
        P("leaf", "col", "row"),
        P("leaf", None),
        P(),
        P(("leaf", "row", "col"), None),
    )
    out_specs = (P("leaf", None, ("col", "row")), P(None, ("leaf", "row", "col")))
    return jax.shard_map(body, mesh=mesh, in_specs=in_specs, out_specs=out_specs, check_vma=False)
```

```python
import functools

import jax
import jax.numpy as jnp
from jax import lax
from jax.experimental import pallas as pl
from jax.experimental.pallas import tpu as pltpu
from jax.sharding import PartitionSpec as P

BLOCK = 128
NZ, NX, NC, NY = 8, 4, 16, 8
F32 = jnp.float32
BF16 = jnp.bfloat16
NT = (((1,), (1,)), ((), ()))
NN = (((1,), (0,)), ((), ()))

COL_STEPS = [(dy, dc) for dy in (4, 3, 5, 2, 6, 1, 7, 0) for dc in (0, 1) if (dy, dc) != (0, 0)]
Z_STEPS = (4, 3, 5, 2, 6, 1, 7)
X_STEPS = (2, 1, 3)


def halves(a):
    hi = a.astype(BF16)
    return hi, (a - hi.astype(F32)).astype(BF16)


def dot3(a, b_hi, b_lo, dims):
    m = a.shape[0]
    a_hi, a_lo = halves(a)
    both = lax.dot_general(jnp.concatenate([a_hi, a_lo], axis=0), b_hi, dims, preferred_element_type=F32)
    rest = lax.dot_general(a_hi, b_lo, dims, preferred_element_type=F32)
    return both[:m] + (both[m:] + rest)


def kernel(
    map_hbm, rhs_hbm, l_hbm, u_hbm, srhs_hbm, s_hbm, leaf_out, sep_out,
    map_ref, rhs_v, l_v, u_v, srhs_v, l_hi, l_lo, u_hi, u_lo, s_v, s_hi, s_lo,
    part, a_rs, fwd, xs, b1, b2, b3s, b3, c_ar, d_ar, e1, e2s, e2, fs, f_rs, red, gs, g_rs,
    load_sem, send_sem, recv_sem,
):
    z = lax.axis_index("leaf")
    x = lax.axis_index("row")
    me = lax.axis_index("col")
    y = me // 2
    core = me % 2

    def col_peer(step):
        return lax.rem(y + step[0], NY) * 2 + lax.rem(core + step[1], 2)

    def z_peer(step):
        return lax.rem(z + step, NZ)

    def x_peer(step):
        return lax.rem(x + step, NX)

    loads = [
        pltpu.make_async_copy(rhs_hbm, rhs_v, load_sem.at[0]),
        *(
            pltpu.make_async_copy(
                l_hbm.at[s, pl.ds(h * 512, 512)], l_v.at[s, pl.ds(h * 512, 512)], load_sem.at[1 + 2 * s + h]
            )
            for s in range(2)
            for h in range(2)
        ),
        pltpu.make_async_copy(u_hbm, u_v, load_sem.at[5]),
        pltpu.make_async_copy(s_hbm.at[:, pl.ds(pl.multiple_of(z * 512, 512), 512)], s_v.at[x, z], load_sem.at[6]),
        pltpu.make_async_copy(srhs_hbm.at[:, pl.ds(pl.multiple_of(z * 512, 512), 512)], srhs_v, load_sem.at[7]),
        pltpu.make_async_copy(map_hbm, map_ref, load_sem.at[8]),
    ]
    for copy in loads:
        copy.start()

    barrier = pltpu.get_barrier_semaphore()
    for step in COL_STEPS:
        pl.semaphore_signal(barrier, inc=1, device_id={"col": col_peer(step)}, device_id_type=pl.DeviceIdType.MESH)
    for step in Z_STEPS:
        pl.semaphore_signal(barrier, inc=1, device_id={"leaf": z_peer(step)}, device_id_type=pl.DeviceIdType.MESH)
    for step in X_STEPS:
        pl.semaphore_signal(barrier, inc=1, device_id={"row": x_peer(step)}, device_id_type=pl.DeviceIdType.MESH)

    def send(stage, src, dst, where):
        pltpu.make_async_remote_copy(
            src_ref=src, dst_ref=dst, send_sem=send_sem.at[stage], recv_sem=recv_sem.at[stage],
            device_id=where, device_id_type=pl.DeviceIdType.MESH,
        ).start()

    def landed(stage, buf, count):
        view = buf.at[pl.ds(0, count)]
        pltpu.make_async_copy(view, view, recv_sem.at[stage]).wait()

    def drained(stage, buf, count):
        view = buf.at[pl.ds(0, count)]
        pltpu.make_async_copy(view, view, send_sem.at[stage]).wait()

    loads[0].wait()
    for s in range(2):
        for h in range(2):
            loads[1 + 2 * s + h].wait()
            rows = pl.ds(h * 512, 512)
            hi, lo = halves(l_v[s, rows])
            l_hi[s, rows] = hi
            l_lo[s, rows] = lo
            p = dot3(rhs_v[s], hi, lo, NT)
            for j in range(4):
                part[2 * (4 * h + j) + s] = p[:, j * 128:(j + 1) * 128]

    pl.semaphore_wait(barrier, len(COL_STEPS) + len(Z_STEPS) + len(X_STEPS))
    for step in COL_STEPS:
        peer = col_peer(step)
        send(0, part.at[peer], a_rs.at[me], {"col": peer})
    for step in Z_STEPS:
        peer = z_peer(step)
        send(1, s_hbm.at[:, pl.ds(pl.multiple_of(peer * 512, 512), 512)], s_v.at[x, z], {"leaf": peer})
    a_rs[me] = part[me]
    loads[5].wait()
    for s in range(2):
        hi, lo = halves(u_v[s])
        u_hi[s] = hi
        u_lo[s] = lo
    landed(0, a_rs, 15)
    fwd[me] = jnp.sum(a_rs[...], axis=0)
    for step in COL_STEPS:
        peer = col_peer(step)
        send(2, fwd.at[me], fwd.at[me], {"col": peer})

    loads[6].wait()
    view = s_v.at[0, pl.ds(0, 7)]
    pltpu.make_async_copy(view, view, recv_sem.at[1]).wait()
    for step in X_STEPS:
        send(3, s_v.at[x], s_v.at[x], {"row": x_peer(step)})

    loads[7].wait()
    loads[8].wait()
    srhs4 = jnp.zeros((4, 512), F32)
    for k in range(NX):
        srhs4 = srhs4 + jnp.where(x == k, srhs_v[4 * k:4 * k + 4, :], 0.0)
    low = lax.broadcasted_iota(jnp.int32, (8, 128), 0) < 4

    landed(2, fwd, 15)
    coupled = []
    for s in range(2):
        f = jnp.concatenate([fwd[2 * j + s] for j in range(8)], axis=1)
        coupled.append(dot3(f, u_hi[s], u_lo[s], NT))
    for k in range(NX):
        xs[k] = jnp.concatenate([coupled[0][4 * k:4 * k + 4], coupled[1][4 * k:4 * k + 4]], axis=0)
    for step in X_STEPS:
        peer = x_peer(step)
        send(4, xs.at[peer], b1.at[x], {"row": peer})
    b1[x] = xs[x]
    landed(4, b1, 3)
    b2[me] = jnp.sum(b1[...], axis=0)
    for step in COL_STEPS:
        send(5, b2.at[me], b2.at[me], {"col": col_peer(step)})

    landed(3, s_v, 3)
    for k in range(NX):
        hi, lo = halves(s_v[k].reshape(64, 512))
        s_hi[k * 64:(k + 1) * 64] = hi
        s_lo[k * 64:(k + 1) * 64] = lo
    which = [jnp.where(low, map_ref[0, k], map_ref[1, k]) for k in range(NC)]

    landed(5, b2, 15)
    tiles = [b2[k] for k in range(NC)]
    for b in range(0, 32, 2):
        pair = []
        for block in (b, b + 1):
            acc = jnp.where(which[0] == block, tiles[0], 0.0)
            for k in range(1, NC):
                acc = acc + jnp.where(which[k] == block, tiles[k], 0.0)
            pair.append(acc + pltpu.roll(acc, 4, 0))
        b3s[b // 4, (b // 2) % 2] = jnp.where(low, pair[0], pair[1])
    for step in Z_STEPS:
        peer = z_peer(step)
        send(6, b3s.at[peer], b3.at[z], {"leaf": peer})
    b3[z] = b3s[z]
    landed(6, b3, 7)
    scattered = jnp.sum(b3[...], axis=0)
    updated = srhs4 - jnp.concatenate(
        [scattered[0, 0:4], scattered[0, 4:8], scattered[1, 0:4], scattered[1, 4:8]], axis=1
    )
    sf = dot3(updated, s_hi[...], s_lo[...], NT)
    c_ar[z] = jnp.concatenate([sf[:, :128], sf[:, 128:]], axis=0)
    for step in Z_STEPS:
        send(7, c_ar.at[z], c_ar.at[z], {"leaf": z_peer(step)})
    landed(7, c_ar, 7)
    sf = jnp.sum(c_ar[...], axis=0)
    sf = jnp.concatenate([sf[0:4], sf[4:8]], axis=1)
    back = dot3(sf, s_hi[...], s_lo[...], NN)
    for p in range(2):
        d_ar[me, p] = jnp.concatenate(
            [back[:, p * 256:p * 256 + 128], back[:, p * 256 + 128:p * 256 + 256]], axis=0
        )
    for step in COL_STEPS:
        send(8, d_ar.at[me], d_ar.at[me], {"col": col_peer(step)})
    landed(8, d_ar, 15)
    sol = jnp.sum(d_ar[...], axis=0)
    e1[z] = sol
    for step in Z_STEPS:
        send(9, e1.at[z], e1.at[z], {"leaf": z_peer(step)})
    for k in range(NX):
        half = sol[k // 2, 4 * (k % 2):4 * (k % 2) + 4]
        e2s[k, 1] = jnp.concatenate([half, half], axis=0)
    landed(9, e1, 7)
    picked = []
    for s in range(2):
        target = map_ref[s, me]
        acc = jnp.zeros((8, 128), F32)
        for q in range(16):
            block = jnp.where(low, 2 * q, 2 * q + 1)
            acc = acc + jnp.where(block == target, e1[q // 2, q % 2], 0.0)
        picked.append(acc + pltpu.roll(acc, 4, 0))
    pulled_tile = jnp.where(low, picked[0], picked[1])
    for k in range(NX):
        e2s[k, 0] = pulled_tile
    for step in X_STEPS:
        peer = x_peer(step)
        send(10, e2s.at[peer], e2.at[x], {"row": peer})
    e2[x] = e2s[x]
    landed(10, e2, 3)
    for s in range(2):
        pulled = jnp.concatenate([e2[k, 0, 4 * s:4 * s + 4] for k in range(NX)], axis=0)
        p = dot3(pulled, u_hi[s], u_lo[s], NN)
        for j in range(8):
            fs[2 * j + s] = p[:, j * 128:(j + 1) * 128]
    for step in COL_STEPS:
        peer = col_peer(step)
        send(11, fs.at[peer], f_rs.at[me], {"col": peer})
    f_rs[me] = fs[me]
    block = jnp.concatenate([e2[k, 1, 0:4] for k in range(NX)], axis=0)
    sep_out[...] = jnp.transpose(pltpu.roll(block, lax.rem(128 - 8 * me, 128), 1))[:8]
    landed(11, f_rs, 15)
    red[me] = fwd[me] - jnp.sum(f_rs[...], axis=0)
    for step in COL_STEPS:
        send(12, red.at[me], red.at[me], {"col": col_peer(step)})
    landed(12, red, 15)
    lp = []
    for s in range(2):
        f = jnp.concatenate([red[2 * j + s] for j in range(8)], axis=1)
        lp.append(dot3(f, l_hi[s], l_lo[s], NN))
    for k in range(NX):
        gs[k] = jnp.concatenate([lp[0][:, k * 64:(k + 1) * 64], lp[1][:, k * 64:(k + 1) * 64]], axis=1)
    for step in X_STEPS:
        peer = x_peer(step)
        send(13, gs.at[peer], g_rs.at[x], {"row": peer})
    g_rs[x] = gs[x]
    drained(0, part, 15)
    view = s_v.at[0, pl.ds(0, 7)]
    pltpu.make_async_copy(view, view, send_sem.at[1]).wait()
    drained(2, fwd, 15)
    drained(3, s_v, 3)
    drained(4, xs, 3)
    drained(5, b2, 15)
    drained(6, b3s, 7)
    drained(7, c_ar, 7)
    drained(8, d_ar, 15)
    drained(9, e1, 7)
    drained(10, e2s, 3)
    drained(11, fs, 15)
    drained(12, red, 15)
    landed(13, g_rs, 3)
    total = jnp.sum(g_rs[...], axis=0)
    leaf_out[0] = total[:, :64]
    leaf_out[1] = total[:, 64:]
    drained(13, gs, 3)


def finish(leaf_in, sep_in, leaf_out, sep_out):
    leaf_out[...] = leaf_in[...]
    sep_out[...] = sep_in[...]


def body(leaf_rhs, leaf_inverse, update_rows, update_map, sep_rhs, sep_inverse):
    hbm = pl.BlockSpec(memory_space=pl.ANY)
    vmem = pl.BlockSpec(memory_space=pltpu.VMEM)
    stages = 14
    leaf, sep = pl.pallas_call(
        kernel,
        name="substitution",
        out_shape=(pltpu.VMEM((2, 16, 64), F32), pltpu.VMEM((8, 16), F32)),
        in_specs=[hbm, hbm, hbm, hbm, hbm, hbm],
        out_specs=(vmem, vmem),
        scratch_shapes=[
            pltpu.SMEM((2, 16), jnp.int32),
            pltpu.VMEM((2, 16, 256), F32),
            pltpu.VMEM((2, 1024, 256), F32),
            pltpu.VMEM((2, 128, 1024), F32),
            pltpu.VMEM((16, 512), F32),
            pltpu.VMEM((2, 1024, 256), BF16),
            pltpu.VMEM((2, 1024, 256), BF16),
            pltpu.VMEM((2, 128, 1024), BF16),
            pltpu.VMEM((2, 128, 1024), BF16),
            pltpu.VMEM((NX, NZ, 8, 512), F32),
            pltpu.VMEM((256, 512), BF16),
            pltpu.VMEM((256, 512), BF16),
            pltpu.VMEM((NC, 16, 128), F32),
            pltpu.VMEM((NC, 16, 128), F32),
            pltpu.VMEM((NC, 16, 128), F32),
            pltpu.VMEM((NX, 8, 128), F32),
            pltpu.VMEM((NX, 8, 128), F32),
            pltpu.VMEM((NC, 8, 128), F32),
            pltpu.VMEM((NZ, 2, 8, 128), F32),
            pltpu.VMEM((NZ, 2, 8, 128), F32),
            pltpu.VMEM((NZ, 8, 128), F32),
            pltpu.VMEM((NC, 2, 8, 128), F32),
            pltpu.VMEM((NZ, 2, 8, 128), F32),
            pltpu.VMEM((NX, 2, 8, 128), F32),
            pltpu.VMEM((NX, 2, 8, 128), F32),
            pltpu.VMEM((NC, 16, 128), F32),
            pltpu.VMEM((NC, 16, 128), F32),
            pltpu.VMEM((NC, 16, 128), F32),
            pltpu.VMEM((NX, 16, 128), F32),
            pltpu.VMEM((NX, 16, 128), F32),
            pltpu.SemaphoreType.DMA((9,)),
            pltpu.SemaphoreType.DMA((stages,)),
            pltpu.SemaphoreType.DMA((stages,)),
        ],
        compiler_params=pltpu.CompilerParams(collective_id=0, has_side_effects=True),
    )(update_map, leaf_rhs, leaf_inverse, update_rows, sep_rhs, sep_inverse)
    leaf, sep = pl.pallas_call(
        finish,
        name="finish",
        out_shape=(jax.ShapeDtypeStruct((2, 16, 64), F32), jax.ShapeDtypeStruct((8, 16), F32)),
        in_specs=[vmem, vmem],
        out_specs=(vmem, vmem),
    )(pltpu.with_memory_space_constraint(leaf, pltpu.VMEM), pltpu.with_memory_space_constraint(sep, pltpu.VMEM))
    return leaf, sep.T


def solution(mesh):
    in_specs = (
        P("leaf", None, "col"),
        P("leaf", "row", "col"),
        P("leaf", "col", "row"),
        P("leaf", None),
        P(),
        P(("leaf", "row", "col"), None),
    )
    out_specs = (P("leaf", None, ("col", "row")), P(None, ("leaf", "row", "col")))
    return jax.shard_map(body, mesh=mesh, in_specs=in_specs, out_specs=out_specs, check_vma=False)
```

```python
import jax
import jax.numpy as jnp
from jax import lax
from jax.experimental import pallas as pl
from jax.experimental.pallas import tpu as pltpu
from jax.sharding import PartitionSpec as P

NZ, NX, NC, NY = 8, 4, 16, 8
F32 = jnp.float32
BF16 = jnp.bfloat16
NT = (((1,), (1,)), ((), ()))
NN = (((1,), (0,)), ((), ()))

Y_STEPS = (4, 3, 5, 2, 6, 1, 7)
COL_STEPS = [(dy, dc) for dy in Y_STEPS + (0,) for dc in (0, 1) if (dy, dc) != (0, 0)]
Z_STEPS = (4, 3, 5, 2, 6, 1, 7)
X_STEPS = (2, 1, 3)
MESH = pl.DeviceIdType.MESH

(A_SUM, S_NEAR, A_GATHER, S_FAR, C_SUM, C_GATHER, S_SWAP, Z_SUM, D_SUM, U_SWAP, D_ROW, F_SUM, F_GATHER, G_SUM,
 L_SWAP, H_ROW, H_COL) = range(17)


def halves(a):
    hi = a.astype(BF16)
    return hi, (a - hi.astype(F32)).astype(BF16)


def dot3(a, b_hi, b_lo, dims):
    m = a.shape[0]
    a_hi, a_lo = halves(a)
    both = lax.dot_general(jnp.concatenate([a_hi, a_lo], axis=0), b_hi, dims, preferred_element_type=F32)
    rest = lax.dot_general(a_hi, b_lo, dims, preferred_element_type=F32)
    return both[:m] + (both[m:] + rest)


def kernel(
    map_hbm, rhs_hbm, l_hbm, u_hbm, srhs_hbm, s_hbm, leaf_out, sep_out,
    map_ref, rhs_v, l_v, l_par, u_own, u_par, srhs_v, l_hi, l_lo, lp_hi, lp_lo, u_hi, u_lo, s_v, s_hi, s_lo,
    part, a_rs, fwd, b1, b2s, b2, c_ar, bs, d_rs, e2, fs, f_rs, red, gs, g_rs, hs, h1, h2,
    load_sem, send_sem, recv_sem,
):
    z = lax.axis_index("leaf")
    x = lax.axis_index("row")
    me = lax.axis_index("col")
    y = me // 2
    core = me % 2
    other = 1 - core
    partner = 2 * y + other

    def col_peer(step):
        return lax.rem(y + step[0], NY) * 2 + lax.rem(core + step[1], 2)

    def y_peer(step):
        return lax.rem(y + step, NY)

    def z_peer(step):
        return lax.rem(z + step, NZ)

    def x_peer(step):
        return lax.rem(x + step, NX)

    s_here = pl.ds(pl.multiple_of(z * 512, 512), 512)
    loads = [
        pltpu.make_async_copy(rhs_hbm, rhs_v, load_sem.at[0]),
        *(
            pltpu.make_async_copy(
                l_hbm.at[s, pl.ds(h * 512, 512)], l_v.at[s, pl.ds(h * 512, 512)], load_sem.at[1 + 2 * s + h]
            )
            for s in range(2)
            for h in range(2)
        ),
        pltpu.make_async_copy(u_hbm.at[core], u_own, load_sem.at[5]),
        pltpu.make_async_copy(s_hbm, s_v.at[core, z], load_sem.at[6]),
        pltpu.make_async_copy(srhs_hbm.at[pl.ds(pl.multiple_of(core * 8, 8), 8), s_here], srhs_v, load_sem.at[7]),
        pltpu.make_async_copy(map_hbm, map_ref, load_sem.at[8]),
    ]
    for copy in loads:
        copy.start()

    barrier = pltpu.get_barrier_semaphore()
    peers = [{"col": col_peer(step)} for step in COL_STEPS]
    peers += [{"leaf": z_peer(step)} for step in Z_STEPS]
    peers += [{"row": x_peer(step)} for step in X_STEPS]
    peers += [{"row": x_peer(step), "col": partner} for step in X_STEPS]
    for peer in peers:
        pl.semaphore_signal(barrier, inc=1, device_id=peer, device_id_type=MESH)

    def send(stage, src, dst, where):
        pltpu.make_async_remote_copy(
            src_ref=src, dst_ref=dst, send_sem=send_sem.at[stage], recv_sem=recv_sem.at[stage],
            device_id=where, device_id_type=MESH,
        ).start()

    def landed(stage, view):
        pltpu.make_async_copy(view, view, recv_sem.at[stage]).wait()

    def drained(stage, view):
        pltpu.make_async_copy(view, view, send_sem.at[stage]).wait()

    loads[0].wait()
    for s in range(2):
        for h in range(2):
            loads[1 + 2 * s + h].wait()
            rows = pl.ds(h * 512, 512)
            hi, lo = halves(l_v[s, rows])
            l_hi[s, rows] = hi
            l_lo[s, rows] = lo
            p = dot3(rhs_v[s], hi, lo, NT)
            for j in range(4):
                part[2 * (4 * h + j) + s] = p[:, j * 128:(j + 1) * 128]

    pl.semaphore_wait(barrier, len(peers))
    for step in COL_STEPS:
        peer = col_peer(step)
        send(A_SUM, part.at[peer], a_rs.at[me], {"col": peer})
    send(U_SWAP, u_hbm.at[other], u_par, {"col": partner})
    for step in (1, 7, 2, 6):
        send(S_NEAR, s_hbm, s_v.at[core, z], {"leaf": z_peer(step)})
    send(S_SWAP, s_hbm, s_v.at[core, z], {"col": partner})
    a_rs[me] = part[me]
    loads[5].wait()
    hi, lo = halves(u_own[...])
    u_hi[0:128] = hi
    u_lo[0:128] = lo
    landed(U_SWAP, u_par)
    hi, lo = halves(u_par[...])
    u_hi[128:256] = hi
    u_lo[128:256] = lo

    landed(A_SUM, a_rs.at[pl.ds(0, 15)])
    fwd[y] = jnp.sum(a_rs[...], axis=0)
    for step in Y_STEPS:
        send(A_GATHER, fwd.at[y], fwd.at[y], {"col": 2 * y_peer(step) + core})
    send(L_SWAP, l_hbm.at[other], l_par, {"col": partner})
    loads[6].wait()
    loads[7].wait()
    loads[8].wait()

    landed(A_GATHER, fwd.at[pl.ds(0, 7)])
    f = jnp.concatenate([fwd[j] for j in range(8)], axis=1)
    coupled = dot3(f, u_hi[...], u_lo[...], NT)
    for q in range(2):
        b1[x, q] = coupled[:, q * 128:(q + 1) * 128]
    for step in X_STEPS:
        send(C_SUM, b1.at[x], b1.at[x], {"row": x_peer(step)})

    landed(S_NEAR, s_v.at[0, pl.ds(0, 4)])
    below = z_peer(6)
    above = z_peer(2)
    send(S_FAR, s_v.at[core, below], s_v.at[core, below], {"leaf": z_peer(1)})
    send(S_FAR, s_v.at[core, above], s_v.at[core, above], {"leaf": z_peer(7)})
    left = pl.ds(0, 2048)
    right = pl.ds(2048, 2048)
    send(S_FAR, s_v.at[core, below, :, left], s_v.at[core, below, :, left], {"leaf": z_peer(2)})
    send(S_FAR, s_v.at[core, above, :, right], s_v.at[core, above, :, right], {"leaf": z_peer(6)})
    for step in (1, 7, 2, 6):
        where = z_peer(step)
        send(S_SWAP, s_v.at[core, where], s_v.at[core, where], {"col": partner})

    landed(C_SUM, b1.at[pl.ds(0, 3)])
    total = jnp.sum(b1[...], axis=0)
    for h in range(2):
        for q in range(2):
            b2s[h, q] = total[q, 8 * h:8 * h + 8]
    for step in COL_STEPS:
        peer = col_peer(step)
        send(C_GATHER, b2s.at[lax.rem(core + step[1], 2)], b2.at[me], {"col": peer})
    b2[me] = b2s[core]

    landed(S_FAR, s_v.at[0, pl.ds(0, 3)])
    for step in (3, 5, 4):
        where = z_peer(step)
        send(S_SWAP, s_v.at[core, where], s_v.at[core, where], {"col": partner})
    landed(S_SWAP, s_v.at[0])
    for b in range(32):
        hi, lo = halves(s_v[:, :, :, b * 128:(b + 1) * 128].reshape(128, 128))
        s_hi[b] = hi
        s_lo[b] = lo

    def block_pair(k):
        c = k % 2
        return map_ref[c, k], map_ref[c, k + 1 - 2 * c]

    def s_pair(ref, pair):
        return jnp.concatenate([ref[pair[0]], ref[pair[1]]], axis=1)

    acc = jnp.zeros((8, 128), F32)
    for i in range(2):
        pair = (4 * z + 2 * i, 4 * z + 2 * i + 1)
        acc = acc + dot3(srhs_v[:, i * 256:(i + 1) * 256], s_pair(s_hi, pair), s_pair(s_lo, pair), NT)

    landed(C_GATHER, b2.at[pl.ds(0, 15)])
    for k in range(NC):
        pair = block_pair(k)
        raw = jnp.concatenate([b2[k, 0], b2[k, 1]], axis=1)
        acc = acc - dot3(raw, s_pair(s_hi, pair), s_pair(s_lo, pair), NT)
    c_ar[z] = acc
    for step in Z_STEPS:
        send(Z_SUM, c_ar.at[z], c_ar.at[z], {"leaf": z_peer(step)})
    landed(L_SWAP, l_par)
    hi, lo = halves(l_par[...])
    lp_hi[...] = hi
    lp_lo[...] = lo
    landed(Z_SUM, c_ar.at[pl.ds(0, 7)])
    sf = jnp.sum(c_ar[...], axis=0)

    for k in range(NC):
        pair = block_pair(k)
        p = dot3(sf, s_pair(s_hi, pair), s_pair(s_lo, pair), NN)
        bs[k, 0] = p[:, :128]
        bs[k, 1] = p[:, 128:]
    for step in COL_STEPS:
        peer = col_peer(step)
        send(D_SUM, bs.at[peer], d_rs.at[me], {"col": peer})
    d_rs[me] = bs[me]
    for i in range(2):
        pair = (4 * z + 2 * i, 4 * z + 2 * i + 1)
        p = dot3(sf, s_pair(s_hi, pair), s_pair(s_lo, pair), NN)
        hs[2 * i] = p[:, :128]
        hs[2 * i + 1] = p[:, 128:]
    for step in X_STEPS:
        peer = x_peer(step)
        send(H_ROW, hs.at[peer], h1.at[x], {"row": peer})
    h1[x] = hs[x]
    landed(H_ROW, h1.at[pl.ds(0, 3)])
    h2[me] = jnp.sum(h1[...], axis=0)

    landed(D_SUM, d_rs.at[pl.ds(0, 15)])
    for h in range(2):
        half = d_rs[h]
        for k in range(1, NY):
            half = half + d_rs[2 * k + h]
        for q in range(2):
            e2[x, q, 8 * h:8 * h + 8] = half[q]
    for step in X_STEPS:
        send(D_ROW, e2.at[x], e2.at[x], {"row": x_peer(step)})
    for step in COL_STEPS:
        send(H_COL, h2.at[me], h2.at[me], {"col": col_peer(step)})
    landed(D_ROW, e2.at[pl.ds(0, 3)])
    pulled = jnp.sum(e2[...], axis=0)
    p = dot3(jnp.concatenate([pulled[0], pulled[1]], axis=1), u_hi[...], u_lo[...], NN)
    for j in range(8):
        fs[j] = p[:, j * 128:(j + 1) * 128]
    for step in Y_STEPS:
        peer = y_peer(step)
        send(F_SUM, fs.at[peer], f_rs.at[y], {"col": 2 * peer + core})
    f_rs[y] = fs[y]
    landed(H_COL, h2.at[pl.ds(0, 15)])
    block = []
    for h in range(2):
        half = h2[h]
        for k in range(1, NY):
            half = half + h2[2 * k + h]
        block.append(half)
    block = jnp.concatenate(block, axis=0)
    sep_out[...] = jnp.transpose(pltpu.roll(block, lax.rem(128 - 8 * me, 128), 1))[:8]
    landed(F_SUM, f_rs.at[pl.ds(0, 7)])
    red[y] = fwd[y] - jnp.sum(f_rs[...], axis=0)
    for step in Y_STEPS:
        send(F_GATHER, red.at[y], red.at[y], {"col": 2 * y_peer(step) + core})
    landed(F_GATHER, red.at[pl.ds(0, 7)])
    f = jnp.concatenate([red[j] for j in range(8)], axis=1)
    for where, mine in ((other, False), (core, True)):
        p = dot3(f, l_hi[core], l_lo[core], NN) if mine else dot3(f, lp_hi[...], lp_lo[...], NN)
        for k in range(NX):
            piece = p[:, k * 64:(k + 1) * 64]
            gs[k, where] = jnp.concatenate([piece[:8], piece[8:]], axis=1)
        for step in X_STEPS:
            peer = x_peer(step)
            send(G_SUM, gs.at[peer, where], g_rs.at[x, core], {"row": peer} if mine else {"row": peer, "col": partner})
    send(G_SUM, gs.at[x, other], g_rs.at[x, core], {"col": partner})
    g_rs[x, core] = gs[x, core]
    drained(A_SUM, part.at[pl.ds(0, 15)])
    drained(S_NEAR, s_v.at[0, pl.ds(0, 4)])
    drained(A_GATHER, fwd.at[pl.ds(0, 7)])
    drained(S_FAR, s_v.at[0, pl.ds(0, 3)])
    drained(C_SUM, b1.at[pl.ds(0, 3)])
    drained(C_GATHER, b2.at[pl.ds(0, 15)])
    drained(S_SWAP, s_v.at[0])
    drained(Z_SUM, c_ar.at[pl.ds(0, 7)])
    drained(D_SUM, d_rs.at[pl.ds(0, 15)])
    drained(U_SWAP, u_par)
    drained(D_ROW, e2.at[pl.ds(0, 3)])
    drained(F_SUM, fs.at[pl.ds(0, 7)])
    drained(F_GATHER, red.at[pl.ds(0, 7)])
    drained(L_SWAP, l_par)
    drained(H_ROW, h1.at[pl.ds(0, 3)])
    drained(H_COL, h2.at[pl.ds(0, 15)])
    landed(G_SUM, c_ar.at[pl.ds(0, 7)])
    total = jnp.sum(g_rs[...], axis=0)
    for s in range(2):
        leaf_out[s, 0:8] = total[s][:, :64]
        leaf_out[s, 8:16] = total[s][:, 64:]
    drained(G_SUM, c_ar.at[pl.ds(0, 7)])


def finish(leaf_in, sep_in, leaf_out, sep_out):
    leaf_out[...] = leaf_in[...]
    sep_out[...] = sep_in[...]


def body(leaf_rhs, leaf_inverse, update_rows, update_map, sep_rhs, sep_inverse):
    hbm = pl.BlockSpec(memory_space=pl.ANY)
    vmem = pl.BlockSpec(memory_space=pltpu.VMEM)
    stages = 17
    leaf, sep = pl.pallas_call(
        kernel,
        name="substitution",
        out_shape=(pltpu.VMEM((2, 16, 64), F32), pltpu.VMEM((8, 16), F32)),
        in_specs=[hbm, hbm, hbm, hbm, hbm, hbm],
        out_specs=(vmem, vmem),
        scratch_shapes=[
            pltpu.SMEM((2, 16), jnp.int32),
            pltpu.VMEM((2, 16, 256), F32),
            pltpu.VMEM((2, 1024, 256), F32),
            pltpu.VMEM((1024, 256), F32),
            pltpu.VMEM((128, 1024), F32),
            pltpu.VMEM((128, 1024), F32),
            pltpu.VMEM((8, 512), F32),
            pltpu.VMEM((2, 1024, 256), BF16),
            pltpu.VMEM((2, 1024, 256), BF16),
            pltpu.VMEM((1024, 256), BF16),
            pltpu.VMEM((1024, 256), BF16),
            pltpu.VMEM((256, 1024), BF16),
            pltpu.VMEM((256, 1024), BF16),
            pltpu.VMEM((2, NZ, 8, 4096), F32),
            pltpu.VMEM((32, 128, 128), BF16),
            pltpu.VMEM((32, 128, 128), BF16),
            pltpu.VMEM((NC, 16, 128), F32),
            pltpu.VMEM((NC, 16, 128), F32),
            pltpu.VMEM((NY, 16, 128), F32),
            pltpu.VMEM((NX, 2, 16, 128), F32),
            pltpu.VMEM((2, 2, 8, 128), F32),
            pltpu.VMEM((NC, 2, 8, 128), F32),
            pltpu.VMEM((NZ, 8, 128), F32),
            pltpu.VMEM((NC, 2, 8, 128), F32),
            pltpu.VMEM((NC, 2, 8, 128), F32),
            pltpu.VMEM((NX, 2, 16, 128), F32),
            pltpu.VMEM((NY, 16, 128), F32),
            pltpu.VMEM((NY, 16, 128), F32),
            pltpu.VMEM((NY, 16, 128), F32),
            pltpu.VMEM((NX, 2, 8, 128), F32),
            pltpu.VMEM((NX, 2, 8, 128), F32),
            pltpu.VMEM((NX, 8, 128), F32),
            pltpu.VMEM((NX, 8, 128), F32),
            pltpu.VMEM((NC, 8, 128), F32),
            pltpu.SemaphoreType.DMA((9,)),
            pltpu.SemaphoreType.DMA((stages,)),
            pltpu.SemaphoreType.DMA((stages,)),
        ],
        compiler_params=pltpu.CompilerParams(collective_id=0, has_side_effects=True),
    )(update_map, leaf_rhs, leaf_inverse, update_rows, sep_rhs, sep_inverse)
    leaf, sep = pl.pallas_call(
        finish,
        name="finish",
        out_shape=(jax.ShapeDtypeStruct((2, 16, 64), F32), jax.ShapeDtypeStruct((8, 16), F32)),
        in_specs=[vmem, vmem],
        out_specs=(vmem, vmem),
    )(pltpu.with_memory_space_constraint(leaf, pltpu.VMEM), pltpu.with_memory_space_constraint(sep, pltpu.VMEM))
    return leaf, sep.T


def solution(mesh):
    in_specs = (
        P("leaf", None, "col"),
        P("leaf", "row", "col"),
        P("leaf", "col", "row"),
        P("leaf", None),
        P(),
        P(("leaf", "row", "col"), None),
    )
    out_specs = (P("leaf", None, ("col", "row")), P(None, ("leaf", "row", "col")))
    return jax.shard_map(body, mesh=mesh, in_specs=in_specs, out_specs=out_specs, check_vma=False)
```

```python
import jax
import jax.numpy as jnp
from jax import lax
from jax.experimental import pallas as pl
from jax.experimental.pallas import tpu as pltpu
from jax.sharding import PartitionSpec as P

NZ, NX, NC, NY = 8, 4, 16, 8
F32 = jnp.float32
BF16 = jnp.bfloat16
NT = (((1,), (1,)), ((), ()))
NN = (((1,), (0,)), ((), ()))

Y_FAR = (4,)
Y_NEAR = (3, 5, 2, 6, 1, 7)
Y_STEPS = Y_FAR + Y_NEAR
COL_FAR = [(4, 0), (4, 1)]
COL_MID = [(dy, dc) for dy in (3, 5) for dc in (0, 1)]
COL_NEAR = [(dy, dc) for dy in (2, 6, 1, 7) for dc in (0, 1)] + [(0, 1)]
COL_STEPS = COL_FAR + COL_MID + COL_NEAR
Z_STEPS = (4, 3, 5, 2, 6, 1, 7)
X_STEPS = (2, 1, 3)
MESH = pl.DeviceIdType.MESH

(A_SUM, S_1, S_2, S_3, S_1B, S_2B, S_3B, S_4, S_SWAP, U_SWAP, L_SWAP, A_FAR, A_NEAR, C_SUM, C_FAR, C_MID, C_NEAR, Z_SUM, D_SUM, D_ROW,
 F_SUM, F_FAR, F_NEAR, G_SUM, H_ROW, H_COL) = range(26)


def halves(a):
    hi = a.astype(BF16)
    return hi, (a - hi.astype(F32)).astype(BF16)


def dot3(a, b_hi, b_lo, dims):
    m = a.shape[0]
    a_hi, a_lo = halves(a)
    both = lax.dot_general(jnp.concatenate([a_hi, a_lo], axis=0), b_hi, dims, preferred_element_type=F32)
    rest = lax.dot_general(a_hi, b_lo, dims, preferred_element_type=F32)
    return both[:m] + (both[m:] + rest)


def kernel(
    map_hbm, rhs_hbm, l_hbm, u_hbm, srhs_hbm, s_hbm, leaf_out, sep_out,
    map_ref, rhs_v, l_v, l_par, u_own, u_par, srhs_v, l_hi, l_lo, lp_hi, lp_lo, u_hi, u_lo, s_v, s_hi, s_lo,
    part, a_rs, fwd, b1, b2s, b2, c_ar, bs, d_rs, e2, fs, f_rs, red, gs, g_rs, hs, h1, h2, hold_a, hold_c, hold_f,
    load_sem, send_sem, recv_sem,
):
    z = lax.axis_index("leaf")
    x = lax.axis_index("row")
    me = lax.axis_index("col")
    y = me // 2
    core = me % 2
    other = 1 - core
    partner = 2 * y + other

    def col_peer(step):
        return lax.rem(y + step[0], NY) * 2 + lax.rem(core + step[1], 2)

    def y_peer(step):
        return lax.rem(y + step, NY)

    def z_peer(step):
        return lax.rem(z + step, NZ)

    def x_peer(step):
        return lax.rem(x + step, NX)

    barrier = pltpu.get_barrier_semaphore()
    peers = [{"col": col_peer(step)} for step in COL_STEPS]
    peers += [{"leaf": z_peer(step)} for step in Z_STEPS]
    peers += [{"row": x_peer(step)} for step in X_STEPS]
    peers += [{"row": x_peer(step), "col": partner} for step in X_STEPS]

    s_here = pl.ds(pl.multiple_of(z * 512, 512), 512)
    loads = [
        pltpu.make_async_copy(rhs_hbm, rhs_v, load_sem.at[0]),
        *(
            pltpu.make_async_copy(
                l_hbm.at[s, pl.ds(h * 512, 512)], l_v.at[s, pl.ds(h * 512, 512)], load_sem.at[1 + 2 * s + h]
            )
            for s in range(2)
            for h in range(2)
        ),
        pltpu.make_async_copy(u_hbm.at[core], u_own, load_sem.at[5]),
        pltpu.make_async_copy(s_hbm, s_v.at[core, z], load_sem.at[6]),
        pltpu.make_async_copy(srhs_hbm.at[pl.ds(pl.multiple_of(core * 8, 8), 8), s_here], srhs_v, load_sem.at[7]),
        pltpu.make_async_copy(map_hbm, map_ref, load_sem.at[8]),
    ]
    for copy in loads[:5]:
        copy.start()
    for peer in peers:
        pl.semaphore_signal(barrier, inc=1, device_id=peer, device_id_type=MESH)
    for copy in loads[5:]:
        copy.start()

    def send(stage, src, dst, where):
        pltpu.make_async_remote_copy(
            src_ref=src, dst_ref=dst, send_sem=send_sem.at[stage], recv_sem=recv_sem.at[stage],
            device_id=where, device_id_type=MESH,
        ).start()

    def landed(stage, view):
        pltpu.make_async_copy(view, view, recv_sem.at[stage]).wait()

    def drained(stage, view):
        pltpu.make_async_copy(view, view, send_sem.at[stage]).wait()

    def split_u(u, row):
        for j in range(8):
            hi, lo = halves(u[:, j * 128:(j + 1) * 128])
            u_hi[j, row:row + 128] = hi
            u_lo[j, row:row + 128] = lo

    loads[0].wait()
    for s in range(2):
        for h in range(2):
            loads[1 + 2 * s + h].wait()
            rows = pl.ds(h * 512, 512)
            hi, lo = halves(l_v[s, rows])
            l_hi[s, rows] = hi
            l_lo[s, rows] = lo
            p = dot3(rhs_v[s], hi, lo, NT)
            for j in range(4):
                part[2 * (4 * h + j) + s] = p[:, j * 128:(j + 1) * 128]

    pl.semaphore_wait(barrier, len(peers))
    for step in COL_STEPS:
        peer = col_peer(step)
        send(A_SUM, part.at[peer], a_rs.at[me], {"col": peer})
    left = pl.ds(0, 2048)
    right = pl.ds(2048, 2048)

    def ring(arrived, onward, columns, distance):
        landed(arrived, s_v.at[0, pl.ds(0, 2), :, columns])
        for step, to in ((distance, 7), (NZ - distance, 1)):
            piece = s_v.at[core, z_peer(step), :, columns]
            if distance < 3:
                send(onward, piece, piece, {"leaf": z_peer(to)})
            elif (columns is left) == (to == 1):
                send(S_4, piece, piece, {"leaf": z_peer(to)})
            send(S_SWAP, piece, piece, {"col": partner})

    send(U_SWAP, u_hbm.at[other], u_par, {"col": partner})
    for stage, columns in ((S_1, left), (S_1B, right)):
        for step in (1, 7):
            send(stage, s_hbm.at[:, columns], s_v.at[core, z, :, columns], {"leaf": z_peer(step)})
    send(S_SWAP, s_hbm, s_v.at[core, z], {"col": partner})
    a_rs[me] = part[me]
    loads[5].wait()
    split_u(u_own, 0)
    landed(U_SWAP, u_par)
    split_u(u_par, 128)

    ring(S_1, S_2, left, 1)
    ring(S_1B, S_2B, right, 1)

    landed(A_SUM, a_rs.at[pl.ds(0, 15)])
    fwd[y] = jnp.sum(a_rs[...], axis=0)
    for stage, steps in ((A_FAR, Y_FAR), (A_NEAR, Y_NEAR)):
        for step in steps:
            send(stage, fwd.at[y], fwd.at[y], {"col": 2 * y_peer(step) + core})
    send(L_SWAP, l_hbm.at[other], l_par, {"col": partner})
    loads[6].wait()
    loads[7].wait()
    loads[8].wait()

    def u_rows(j):
        return u_hi[j], u_lo[j]

    def gathered(vectors, matrix, steps, dims):
        chips = [y_peer(step) for step in steps]
        v = jnp.concatenate([vectors[j] for j in chips], axis=1)
        parts = [matrix(j) for j in chips]
        axis = dims[0][1][0]
        return dot3(
            v, jnp.concatenate([p[0] for p in parts], axis=axis), jnp.concatenate([p[1] for p in parts], axis=axis), dims
        )

    ring(S_2, S_3, left, 2)
    ring(S_2B, S_3B, right, 2)
    landed(A_NEAR, fwd.at[pl.ds(0, 6)])
    coupled = gathered(fwd, u_rows, (0,) + Y_NEAR, NT)
    hold_a[...] = coupled
    landed(A_FAR, fwd.at[pl.ds(0, 1)])
    coupled = hold_a[...] + gathered(fwd, u_rows, Y_FAR, NT)
    for q in range(2):
        b1[x, q] = coupled[:, q * 128:(q + 1) * 128]
    for step in X_STEPS:
        send(C_SUM, b1.at[x], b1.at[x], {"row": x_peer(step)})

    ring(S_3, S_4, left, 3)
    ring(S_3B, S_4, right, 3)

    landed(C_SUM, b1.at[pl.ds(0, 3)])
    total = jnp.sum(b1[...], axis=0)
    for h in range(2):
        for q in range(2):
            b2s[h, q] = total[q, 8 * h:8 * h + 8]
    for stage, steps in ((C_FAR, COL_FAR), (C_MID, COL_MID), (C_NEAR, COL_NEAR)):
        for step in steps:
            send(stage, b2s.at[lax.rem(core + step[1], 2)], b2.at[me], {"col": col_peer(step)})
    b2[me] = b2s[core]

    landed(S_4, s_v.at[0, 0])
    piece = s_v.at[core, z_peer(4)]
    send(S_SWAP, piece, piece, {"col": partner})

    def split_s(c):
        rows = pl.ds(pl.multiple_of(c * 64, 64), 64)
        for b in range(32):
            hi, lo = halves(s_v[c, :, :, b * 128:(b + 1) * 128].reshape(64, 128))
            s_hi[b, rows] = hi
            s_lo[b, rows] = lo

    split_s(core)
    landed(S_SWAP, s_v.at[0])
    split_s(other)

    def block_pair(k):
        c = lax.rem(k, 2)
        return map_ref[c, k], map_ref[c, k + 1 - 2 * c]

    def s_join(ref, blocks):
        return jnp.concatenate([ref[b] for b in blocks], axis=1)

    def s_times(v, blocks, dims):
        return dot3(v, s_join(s_hi, blocks), s_join(s_lo, blocks), dims)

    here = [4 * z + i for i in range(4)]

    def arrived_times_s(steps):
        cols = [col_peer(step) for step in steps]
        raw = jnp.concatenate([b2[k, q] for k in cols for q in range(2)], axis=1)
        return s_times(raw, [b for k in cols for b in block_pair(k)], NT)

    acc = s_times(srhs_v[...], here, NT)
    landed(C_NEAR, b2.at[pl.ds(0, 9)])
    hold_c[...] = acc - arrived_times_s([(0, 0)] + COL_NEAR)
    landed(C_MID, b2.at[pl.ds(0, 4)])
    hold_c[...] = hold_c[...] - arrived_times_s(COL_MID)
    landed(C_FAR, b2.at[pl.ds(0, 2)])
    c_ar[z] = hold_c[...] - arrived_times_s(COL_FAR)
    for step in Z_STEPS:
        send(Z_SUM, c_ar.at[z], c_ar.at[z], {"leaf": z_peer(step)})
    landed(L_SWAP, l_par)
    hi, lo = halves(l_par[...])
    lp_hi[...] = hi
    lp_lo[...] = lo
    landed(Z_SUM, c_ar.at[pl.ds(0, 7)])
    sf = jnp.sum(c_ar[...], axis=0)

    for steps in (COL_FAR + COL_MID, COL_NEAR + [(0, 0)]):
        cols = [col_peer(step) for step in steps]
        p = s_times(sf, [b for k in cols for b in block_pair(k)], NN)
        for i, k in enumerate(cols):
            bs[k, 0] = p[:, 256 * i:256 * i + 128]
            bs[k, 1] = p[:, 256 * i + 128:256 * i + 256]
        for step, k in zip(steps, cols):
            if step != (0, 0):
                send(D_SUM, bs.at[k], d_rs.at[me], {"col": k})
    d_rs[me] = bs[me]
    p = s_times(sf, here, NN)
    for i in range(4):
        hs[i] = p[:, 128 * i:128 * i + 128]
    for step in X_STEPS:
        peer = x_peer(step)
        send(H_ROW, hs.at[peer], h1.at[x], {"row": peer})
    h1[x] = hs[x]
    landed(H_ROW, h1.at[pl.ds(0, 3)])
    h2[me] = jnp.sum(h1[...], axis=0)

    landed(D_SUM, d_rs.at[pl.ds(0, 15)])
    for h in range(2):
        half = d_rs[h]
        for k in range(1, NY):
            half = half + d_rs[2 * k + h]
        for q in range(2):
            e2[x, q, 8 * h:8 * h + 8] = half[q]
    for step in X_STEPS:
        send(D_ROW, e2.at[x], e2.at[x], {"row": x_peer(step)})
    for step in COL_STEPS:
        send(H_COL, h2.at[me], h2.at[me], {"col": col_peer(step)})
    landed(D_ROW, e2.at[pl.ds(0, 3)])
    pulled = jnp.sum(e2[...], axis=0)
    p = dot3(
        jnp.concatenate([pulled[0], pulled[1]], axis=1),
        jnp.concatenate([u_hi[j] for j in range(8)], axis=1), jnp.concatenate([u_lo[j] for j in range(8)], axis=1), NN,
    )
    for j in range(8):
        fs[j] = p[:, j * 128:(j + 1) * 128]
    for step in Y_STEPS:
        peer = y_peer(step)
        send(F_SUM, fs.at[peer], f_rs.at[y], {"col": 2 * peer + core})
    f_rs[y] = fs[y]
    landed(H_COL, h2.at[pl.ds(0, 15)])
    block = []
    for h in range(2):
        half = h2[h]
        for k in range(1, NY):
            half = half + h2[2 * k + h]
        block.append(half)
    block = jnp.concatenate(block, axis=0)
    sep_out[...] = jnp.transpose(pltpu.roll(block, lax.rem(128 - 8 * me, 128), 1))[:8]
    landed(F_SUM, f_rs.at[pl.ds(0, 7)])
    red[y] = fwd[y] - jnp.sum(f_rs[...], axis=0)
    for stage, steps in ((F_FAR, Y_FAR), (F_NEAR, Y_NEAR)):
        for step in steps:
            send(stage, red.at[y], red.at[y], {"col": 2 * y_peer(step) + core})

    def l_partner(j):
        rows = pl.ds(pl.multiple_of(j * 128, 128), 128)
        return lp_hi[rows], lp_lo[rows]

    def l_own(j):
        rows = pl.ds(pl.multiple_of(j * 128, 128), 128)
        return l_hi[core, rows], l_lo[core, rows]

    landed(F_NEAR, red.at[pl.ds(0, 6)])
    for i, matrix in enumerate((l_partner, l_own)):
        hold_f[i] = gathered(red, matrix, (0,) + Y_NEAR, NN)
    landed(F_FAR, red.at[pl.ds(0, 1)])
    for where, mine, matrix in ((other, False, l_partner), (core, True, l_own)):
        p = hold_f[int(mine)] + gathered(red, matrix, Y_FAR, NN)
        for k in range(NX):
            piece = p[:, k * 64:(k + 1) * 64]
            gs[k, where] = jnp.concatenate([piece[:8], piece[8:]], axis=1)
        for step in X_STEPS:
            peer = x_peer(step)
            send(G_SUM, gs.at[peer, where], g_rs.at[x, core], {"row": peer} if mine else {"row": peer, "col": partner})
    send(G_SUM, gs.at[x, other], g_rs.at[x, core], {"col": partner})
    g_rs[x, core] = gs[x, core]
    drained(A_SUM, part.at[pl.ds(0, 15)])
    for stage in (S_1, S_2, S_3):
        drained(stage, s_v.at[0, pl.ds(0, 2), :, left])
    for stage in (S_1B, S_2B, S_3B):
        drained(stage, s_v.at[0, pl.ds(0, 2), :, right])
    drained(S_4, s_v.at[0, 0])
    drained(S_SWAP, s_v.at[0])
    drained(U_SWAP, u_par)
    drained(L_SWAP, l_par)
    drained(A_FAR, fwd.at[pl.ds(0, 1)])
    drained(A_NEAR, fwd.at[pl.ds(0, 6)])
    drained(C_SUM, b1.at[pl.ds(0, 3)])
    drained(C_FAR, b2.at[pl.ds(0, 2)])
    drained(C_MID, b2.at[pl.ds(0, 4)])
    drained(C_NEAR, b2.at[pl.ds(0, 9)])
    drained(Z_SUM, c_ar.at[pl.ds(0, 7)])
    drained(D_SUM, d_rs.at[pl.ds(0, 15)])
    drained(D_ROW, e2.at[pl.ds(0, 3)])
    drained(F_SUM, fs.at[pl.ds(0, 7)])
    drained(F_FAR, red.at[pl.ds(0, 1)])
    drained(F_NEAR, red.at[pl.ds(0, 6)])
    drained(H_ROW, h1.at[pl.ds(0, 3)])
    drained(H_COL, h2.at[pl.ds(0, 15)])
    landed(G_SUM, c_ar.at[pl.ds(0, 7)])
    total = jnp.sum(g_rs[...], axis=0)
    for s in range(2):
        leaf_out[s, 0:8] = total[s][:, :64]
        leaf_out[s, 8:16] = total[s][:, 64:]
    drained(G_SUM, c_ar.at[pl.ds(0, 7)])


def finish(leaf_in, sep_in, leaf_out, sep_out):
    leaf_out[...] = leaf_in[...]
    sep_out[...] = sep_in[...]


def body(leaf_rhs, leaf_inverse, update_rows, update_map, sep_rhs, sep_inverse):
    hbm = pl.BlockSpec(memory_space=pl.ANY)
    vmem = pl.BlockSpec(memory_space=pltpu.VMEM)
    stages = 26
    leaf, sep = pl.pallas_call(
        kernel,
        name="substitution",
        out_shape=(pltpu.VMEM((2, 16, 64), F32), pltpu.VMEM((8, 16), F32)),
        in_specs=[hbm, hbm, hbm, hbm, hbm, hbm],
        out_specs=(vmem, vmem),
        scratch_shapes=[
            pltpu.SMEM((2, 16), jnp.int32),
            pltpu.VMEM((2, 16, 256), F32),
            pltpu.VMEM((2, 1024, 256), F32),
            pltpu.VMEM((1024, 256), F32),
            pltpu.VMEM((128, 1024), F32),
            pltpu.VMEM((128, 1024), F32),
            pltpu.VMEM((8, 512), F32),
            pltpu.VMEM((2, 1024, 256), BF16),
            pltpu.VMEM((2, 1024, 256), BF16),
            pltpu.VMEM((1024, 256), BF16),
            pltpu.VMEM((1024, 256), BF16),
            pltpu.VMEM((NY, 256, 128), BF16),
            pltpu.VMEM((NY, 256, 128), BF16),
            pltpu.VMEM((2, NZ, 8, 4096), F32),
            pltpu.VMEM((32, 128, 128), BF16),
            pltpu.VMEM((32, 128, 128), BF16),
            pltpu.VMEM((NC, 16, 128), F32),
            pltpu.VMEM((NC, 16, 128), F32),
            pltpu.VMEM((NY, 16, 128), F32),
            pltpu.VMEM((NX, 2, 16, 128), F32),
            pltpu.VMEM((2, 2, 8, 128), F32),
            pltpu.VMEM((NC, 2, 8, 128), F32),
            pltpu.VMEM((NZ, 8, 128), F32),
            pltpu.VMEM((NC, 2, 8, 128), F32),
            pltpu.VMEM((NC, 2, 8, 128), F32),
            pltpu.VMEM((NX, 2, 16, 128), F32),
            pltpu.VMEM((NY, 16, 128), F32),
            pltpu.VMEM((NY, 16, 128), F32),
            pltpu.VMEM((NY, 16, 128), F32),
            pltpu.VMEM((NX, 2, 8, 128), F32),
            pltpu.VMEM((NX, 2, 8, 128), F32),
            pltpu.VMEM((NX, 8, 128), F32),
            pltpu.VMEM((NX, 8, 128), F32),
            pltpu.VMEM((NC, 8, 128), F32),
            pltpu.VMEM((16, 256), F32),
            pltpu.VMEM((8, 128), F32),
            pltpu.VMEM((2, 16, 256), F32),
            pltpu.SemaphoreType.DMA((9,)),
            pltpu.SemaphoreType.DMA((stages,)),
            pltpu.SemaphoreType.DMA((stages,)),
        ],
        compiler_params=pltpu.CompilerParams(collective_id=0, has_side_effects=True),
    )(update_map, leaf_rhs, leaf_inverse, update_rows, sep_rhs, sep_inverse)
    leaf, sep = pl.pallas_call(
        finish,
        name="finish",
        out_shape=(jax.ShapeDtypeStruct((2, 16, 64), F32), jax.ShapeDtypeStruct((8, 16), F32)),
        in_specs=[vmem, vmem],
        out_specs=(vmem, vmem),
    )(pltpu.with_memory_space_constraint(leaf, pltpu.VMEM), pltpu.with_memory_space_constraint(sep, pltpu.VMEM))
    return leaf, sep.T


def solution(mesh):
    in_specs = (
        P("leaf", None, "col"),
        P("leaf", "row", "col"),
        P("leaf", "col", "row"),
        P("leaf", None),
        P(),
        P(("leaf", "row", "col"), None),
    )
    out_specs = (P("leaf", None, ("col", "row")), P(None, ("leaf", "row", "col")))
    return jax.shard_map(body, mesh=mesh, in_specs=in_specs, out_specs=out_specs, check_vma=False)
```

```python
import jax
import jax.numpy as jnp
from jax import lax
from jax.experimental import pallas as pl
from jax.experimental.pallas import tpu as pltpu
from jax.sharding import PartitionSpec as P

NZ, NX, NC, NY = 8, 4, 16, 8
F32 = jnp.float32
BF16 = jnp.bfloat16
NT = (((1,), (1,)), ((), ()))
NN = (((1,), (0,)), ((), ()))

Y_GROUPS = ((4,), (3, 5, 2, 6, 1, 7))
Y_STEPS = sum(Y_GROUPS, ())
COL_GROUPS = [[(dy, dc) for dy in steps for dc in (0, 1) if (dy, dc) != (0, 0)] for steps in ((4,), (3, 5, 2, 6, 1, 7, 0))]
COL_STEPS = sum(COL_GROUPS, [])
Z_STEPS = (4, 3, 5, 2, 6, 1, 7)
X_STEPS = (2, 1, 3)
MESH = pl.DeviceIdType.MESH

(A_SUM, S_OWN, S_4, S_SWAP, U_SWAP, L_SWAP, C_SUM, Z_SUM, D_SUM, D_ROW, F_SUM, G_SUM, H_ROW, H_COL) = range(14)
A_GATHER = 14
F_GATHER = 16
C_GATHER = 18
S_RING = 20
STAGES = 32
TILES = 1059


def halves(a):
    hi = a.astype(BF16)
    return hi, (a - hi.astype(F32)).astype(BF16)


def dot3(a, b_hi, b_lo, dims):
    m = a.shape[0]
    a_hi, a_lo = halves(a)
    both = lax.dot_general(jnp.concatenate([a_hi, a_lo], axis=0), b_hi, dims, preferred_element_type=F32)
    rest = lax.dot_general(a_hi, b_lo, dims, preferred_element_type=F32)
    return both[:m] + (both[m:] + rest)


def kernel(
    map_hbm, rhs_hbm, l_hbm, u_hbm, srhs_hbm, s_hbm, leaf_out, sep_out,
    map_ref, rhs_v, l_v, l_par, u_own, u_par, srhs_v, l_hi, l_lo, lp_hi, lp_lo, u_hi, u_lo, ut_hi, ut_lo, s_v, s_hi, s_lo, st_hi, st_lo,
    part, a_rs, fwd, b1, b2s, b2, c_ar, bs, d_rs, e2, fs, f_rs, red, gs, g_rs, hs, h1, h2, hold_a, hold_c, hold_f, tally,
    load_sem, send_sem, recv_sem,
):
    z = lax.axis_index("leaf")
    x = lax.axis_index("row")
    me = lax.axis_index("col")
    y = me // 2
    core = me % 2
    other = 1 - core
    partner = 2 * y + other

    def col_peer(step):
        return lax.rem(y + step[0], NY) * 2 + lax.rem(core + step[1], 2)

    def y_peer(step):
        return lax.rem(y + step, NY)

    def z_peer(step):
        return lax.rem(z + step, NZ)

    def x_peer(step):
        return lax.rem(x + step, NX)

    barrier = pltpu.get_barrier_semaphore()
    peers = [{"leaf": z_peer(step)} for step in (4, 3, 5)]
    peers += [{"col": col_peer(step)} for step in COL_STEPS]
    peers += [{"row": x_peer(step)} for step in X_STEPS]
    peers += [{"row": x_peer(step), "col": partner} for step in X_STEPS]
    peers += [{"leaf": z_peer(step)} for step in (2, 6, 1, 7)]
    for peer in peers:
        pl.semaphore_signal(barrier, inc=1, device_id=peer, device_id_type=MESH)

    s_here = pl.ds(pl.multiple_of(z * 512, 512), 512)
    loads = [
        pltpu.make_async_copy(rhs_hbm, rhs_v, load_sem.at[0]),
        *(
            pltpu.make_async_copy(
                l_hbm.at[s, pl.ds(h * 512, 512)], l_v.at[s, pl.ds(h * 512, 512)], load_sem.at[1 + 2 * s + h]
            )
            for s in range(2)
            for h in range(2)
        ),
        pltpu.make_async_copy(u_hbm.at[core], u_own, load_sem.at[5]),
        pltpu.make_async_copy(s_hbm, s_v.at[z, core], load_sem.at[6]),
        pltpu.make_async_copy(srhs_hbm.at[pl.ds(pl.multiple_of(core * 8, 8), 8), s_here], srhs_v, load_sem.at[7]),
        pltpu.make_async_copy(map_hbm, map_ref, load_sem.at[8]),
    ]
    for copy in loads:
        copy.start()

    def send(stage, src, dst, where):
        pltpu.make_async_remote_copy(
            src_ref=src, dst_ref=dst, send_sem=send_sem.at[0], recv_sem=recv_sem.at[stage],
            device_id=where, device_id_type=MESH,
        ).start()

    def landed(stage, view):
        pltpu.make_async_copy(view, view, recv_sem.at[stage]).wait()

    def split_u(u, row):
        for j in range(8):
            hi, lo = halves(u[:, j * 128:(j + 1) * 128])
            u_hi[j, row:row + 128] = hi
            u_lo[j, row:row + 128] = lo
            hi, lo = halves(jnp.transpose(u[:, j * 128:(j + 1) * 128]))
            ut_hi[j, :, row:row + 128] = hi
            ut_lo[j, :, row:row + 128] = lo

    loads[0].wait()
    for s in range(2):
        for h in range(2):
            loads[1 + 2 * s + h].wait()
            rows = pl.ds(h * 512, 512)
            hi, lo = halves(l_v[s, rows])
            l_hi[s, rows] = hi
            l_lo[s, rows] = lo
            p = dot3(rhs_v[s], hi, lo, NT)
            for j in range(4):
                part[2 * (4 * h + j) + s] = p[:, j * 128:(j + 1) * 128]

    pl.semaphore_wait(barrier, len(peers))
    for step in COL_STEPS:
        peer = col_peer(step)
        send(A_SUM, part.at[peer], a_rs.at[me], {"col": peer})
    onward = lax.rem(z + 2 * core + 7, NZ)
    halved = (pl.ds(0, 2048), pl.ds(2048, 2048))
    pieces = [(owner, columns) for owner in (core, other) for columns in halved]

    def behind(distance):
        return lax.rem(z + NZ + distance * (1 - 2 * core), NZ)

    def ring(distance, i):
        stage = S_RING + 4 * (distance - 1) + i
        owner, columns = pieces[i]
        piece = s_v.at[behind(distance), owner, :, columns]
        landed(stage, s_v.at[0, 0, :, halved[0]])
        if distance < 3:
            send(stage + 4, piece, piece, {"leaf": onward})
        elif i % 2 == 1:
            last_step(owner)
        send(S_SWAP, piece, piece, {"col": partner})

    def last_step(owner):
        piece = s_v.at[behind(3), owner, :, pl.ds(pl.multiple_of(2048 * core, 2048), 2048)]
        send(S_4, piece, piece, {"leaf": onward})

    send(S_OWN, s_hbm, s_v.at[z, core], {"col": partner})
    for i in range(2):
        columns = halved[i]
        send(S_RING + i, s_hbm.at[:, columns], s_v.at[z, core, :, columns], {"leaf": onward})
    send(U_SWAP, u_hbm.at[other], u_par, {"col": partner})
    a_rs[me] = part[me]
    loads[5].wait()
    split_u(u_own, 0)
    landed(S_OWN, s_v.at[0, 0])
    for i in range(2):
        piece = s_v.at[z, other, :, halved[i]]
        send(S_RING + 2 + i, piece, piece, {"leaf": onward})
    landed(U_SWAP, u_par)
    split_u(u_par, 128)

    for i in range(4):
        ring(1, i)

    landed(A_SUM, a_rs.at[pl.ds(0, 15)])
    fwd[y] = jnp.sum(a_rs[...], axis=0)
    for i, steps in enumerate(Y_GROUPS):
        for step in steps:
            send(A_GATHER + i, fwd.at[y], fwd.at[y], {"col": 2 * y_peer(step) + core})
    loads[6].wait()
    loads[7].wait()
    loads[8].wait()

    def u_columns(j):
        return ut_hi[j], ut_lo[j]

    def gathered(vectors, matrix, steps):
        chips = [y_peer(step) for step in steps]
        v = jnp.concatenate([vectors[j] for j in chips], axis=1)
        parts = [matrix(j) for j in chips]
        return dot3(v, *(jnp.concatenate([p[i] for p in parts], axis=0) for i in range(2)), NN)

    for i in range(4):
        ring(2, i)
    landed(A_GATHER + 1, fwd.at[pl.ds(0, 6)])
    hold_a[...] = gathered(fwd, u_columns, (0,) + Y_GROUPS[1])
    landed(A_GATHER, fwd.at[0])
    coupled = hold_a[...] + gathered(fwd, u_columns, Y_GROUPS[0])
    for q in range(2):
        b1[x, q] = coupled[:, q * 128:(q + 1) * 128]
    for step in X_STEPS:
        send(C_SUM, b1.at[x], b1.at[x], {"row": x_peer(step)})

    for i in range(4):
        ring(3, i)

    landed(C_SUM, b1.at[pl.ds(0, 3)])
    total = jnp.sum(b1[...], axis=0)
    for h in range(2):
        for q in range(2):
            b2s[h, q] = total[q, 8 * h:8 * h + 8]
    for i, steps in enumerate(COL_GROUPS):
        for step in steps:
            send(C_GATHER + i, b2s.at[lax.rem(core + step[1], 2)], b2.at[me], {"col": col_peer(step)})
    b2[me] = b2s[core]

    def split_s(where):
        rows = pl.ds(pl.multiple_of(where * 16, 16), 16)
        for b in range(32):
            hi, lo = halves(s_v[where, :, :, b * 128:(b + 1) * 128].reshape(16, 128))
            s_hi[b, rows] = hi
            s_lo[b, rows] = lo

    for distance in range(4):
        split_s(behind(distance))
    landed(S_4, s_v.at[0, 0])
    piece = s_v.at[behind(4), :, :, pl.ds(pl.multiple_of(2048 * core, 2048), 2048)]
    send(S_SWAP, piece, piece, {"col": partner})
    landed(S_SWAP, s_v.at[pl.ds(0, 7), 0])
    for distance in range(4, 8):
        split_s(behind(distance))
    for b in range(32):
        hi, lo = halves(jnp.transpose(s_v[:, :, :, b * 128:(b + 1) * 128].reshape(128, 128)))
        st_hi[b] = hi
        st_lo[b] = lo

    def block_pair(k):
        c = lax.rem(k, 2)
        return map_ref[c, k], map_ref[c, k + 1 - 2 * c]

    def join(ref, blocks, axis):
        return jnp.concatenate([ref[b] for b in blocks], axis=axis)

    def times_st(v, blocks):
        return dot3(v, join(st_hi, blocks, 0), join(st_lo, blocks, 0), NN)

    def times_s(v, blocks):
        return dot3(v, join(s_hi, blocks, 1), join(s_lo, blocks, 1), NN)

    here = [4 * z + i for i in range(4)]

    def arrived_times_s(steps):
        cols = [col_peer(step) for step in steps]
        raw = jnp.concatenate([b2[k, q] for k in cols for q in range(2)], axis=1)
        return times_st(raw, [b for k in cols for b in block_pair(k)])

    hold_c[...] = times_st(srhs_v[...], here) - arrived_times_s([(0, 0)])
    for i, steps in reversed(list(enumerate(COL_GROUPS))):
        landed(C_GATHER + i, b2.at[pl.ds(0, len(steps))])
        hold_c[...] = hold_c[...] - arrived_times_s(steps)
    c_ar[z] = hold_c[...]
    for step in Z_STEPS:
        send(Z_SUM, c_ar.at[z], c_ar.at[z], {"leaf": z_peer(step)})
    send(L_SWAP, l_hbm.at[other], l_par, {"col": partner})
    landed(Z_SUM, c_ar.at[pl.ds(0, 7)])
    sf = jnp.sum(c_ar[...], axis=0)

    for steps in (COL_STEPS[:6], COL_STEPS[6:] + [(0, 0)]):
        cols = [col_peer(step) for step in steps]
        p = times_s(sf, [b for k in cols for b in block_pair(k)])
        for i, k in enumerate(cols):
            bs[k, 0] = p[:, 256 * i:256 * i + 128]
            bs[k, 1] = p[:, 256 * i + 128:256 * i + 256]
        for step, k in zip(steps, cols):
            if step != (0, 0):
                send(D_SUM, bs.at[k], d_rs.at[me], {"col": k})
    d_rs[me] = bs[me]
    p = times_s(sf, here)
    for i in range(4):
        hs[i] = p[:, 128 * i:128 * i + 128]
    for step in X_STEPS:
        peer = x_peer(step)
        send(H_ROW, hs.at[peer], h1.at[x], {"row": peer})
    h1[x] = hs[x]
    landed(H_ROW, h1.at[pl.ds(0, 3)])
    h2[me] = jnp.sum(h1[...], axis=0)

    landed(L_SWAP, l_par)
    hi, lo = halves(l_par[...])
    lp_hi[...] = hi
    lp_lo[...] = lo
    landed(D_SUM, d_rs.at[pl.ds(0, 15)])
    for h in range(2):
        half = d_rs[h]
        for k in range(1, NY):
            half = half + d_rs[2 * k + h]
        for q in range(2):
            e2[x, q, 8 * h:8 * h + 8] = half[q]
    for step in X_STEPS:
        send(D_ROW, e2.at[x], e2.at[x], {"row": x_peer(step)})
    for step in COL_STEPS:
        send(H_COL, h2.at[me], h2.at[me], {"col": col_peer(step)})
    landed(D_ROW, e2.at[pl.ds(0, 3)])
    pulled = jnp.sum(e2[...], axis=0)
    p = dot3(
        jnp.concatenate([pulled[0], pulled[1]], axis=1),
        jnp.concatenate([u_hi[j] for j in range(8)], axis=1), jnp.concatenate([u_lo[j] for j in range(8)], axis=1), NN,
    )
    for j in range(8):
        fs[j] = p[:, j * 128:(j + 1) * 128]
    for step in Y_STEPS:
        peer = y_peer(step)
        send(F_SUM, fs.at[peer], f_rs.at[y], {"col": 2 * peer + core})
    f_rs[y] = fs[y]
    landed(H_COL, h2.at[pl.ds(0, 15)])
    block = []
    for h in range(2):
        half = h2[h]
        for k in range(1, NY):
            half = half + h2[2 * k + h]
        block.append(half)
    block = jnp.concatenate(block, axis=0)
    sep_out[...] = jnp.transpose(pltpu.roll(block, lax.rem(128 - 8 * me, 128), 1))[:8]
    landed(F_SUM, f_rs.at[pl.ds(0, 7)])
    red[y] = fwd[y] - jnp.sum(f_rs[...], axis=0)
    for i, steps in enumerate(Y_GROUPS):
        for step in steps:
            send(F_GATHER + i, red.at[y], red.at[y], {"col": 2 * y_peer(step) + core})

    def l_partner(j):
        rows = pl.ds(pl.multiple_of(j * 128, 128), 128)
        return lp_hi[rows], lp_lo[rows]

    def l_own(j):
        rows = pl.ds(pl.multiple_of(j * 128, 128), 128)
        return l_hi[core, rows], l_lo[core, rows]

    matrices = (l_partner, l_own)
    landed(F_GATHER + 1, red.at[pl.ds(0, 6)])
    for i, matrix in enumerate(matrices):
        hold_f[i] = gathered(red, matrix, (0,) + Y_GROUPS[1])
    landed(F_GATHER, red.at[0])
    for i, (where, matrix) in enumerate(((other, l_partner), (core, l_own))):
        p = hold_f[i] + gathered(red, matrix, Y_GROUPS[0])
        gs[0, where] = p[:, :128]
        gs[1, where] = p[:, 128:]
        for step in X_STEPS:
            peer = x_peer(step)
            to = {"row": peer} if i == 1 else {"row": peer, "col": partner}
            send(G_SUM, gs.at[peer // 2, where], g_rs.at[x, core], to)
    send(G_SUM, gs.at[x // 2, other], g_rs.at[x, core], {"col": partner})
    g_rs[x, core] = gs[x // 2, core]
    landed(G_SUM, fs.at[pl.ds(0, 7)])
    total = jnp.sum(g_rs[...], axis=0)
    for s in range(2):
        leaf_out[s] = jnp.where(lax.rem(x, 2) == 0, total[s][:, :64], total[s][:, 64:])
    pltpu.make_async_copy(tally, tally, send_sem.at[0]).wait()


def finish(leaf_in, sep_in, leaf_out, sep_out):
    leaf_out[...] = leaf_in[...]
    sep_out[...] = sep_in[...]


def body(leaf_rhs, leaf_inverse, update_rows, update_map, sep_rhs, sep_inverse):
    hbm = pl.BlockSpec(memory_space=pl.ANY)
    vmem = pl.BlockSpec(memory_space=pltpu.VMEM)
    leaf, sep = pl.pallas_call(
        kernel,
        name="substitution",
        out_shape=(pltpu.VMEM((2, 16, 64), F32), pltpu.VMEM((8, 16), F32)),
        in_specs=[hbm, hbm, hbm, hbm, hbm, hbm],
        out_specs=(vmem, vmem),
        scratch_shapes=[
            pltpu.SMEM((2, 16), jnp.int32),
            pltpu.VMEM((2, 16, 256), F32),
            pltpu.VMEM((2, 1024, 256), F32),
            pltpu.VMEM((1024, 256), F32),
            pltpu.VMEM((128, 1024), F32),
            pltpu.VMEM((128, 1024), F32),
            pltpu.VMEM((8, 512), F32),
            pltpu.VMEM((2, 1024, 256), BF16),
            pltpu.VMEM((2, 1024, 256), BF16),
            pltpu.VMEM((1024, 256), BF16),
            pltpu.VMEM((1024, 256), BF16),
            pltpu.VMEM((NY, 256, 128), BF16),
            pltpu.VMEM((NY, 256, 128), BF16),
            pltpu.VMEM((NY, 128, 256), BF16),
            pltpu.VMEM((NY, 128, 256), BF16),
            pltpu.VMEM((NZ, 2, 8, 4096), F32),
            pltpu.VMEM((32, 128, 128), BF16),
            pltpu.VMEM((32, 128, 128), BF16),
            pltpu.VMEM((32, 128, 128), BF16),
            pltpu.VMEM((32, 128, 128), BF16),
            pltpu.VMEM((NC, 16, 128), F32),
            pltpu.VMEM((NC, 16, 128), F32),
            pltpu.VMEM((NY, 16, 128), F32),
            pltpu.VMEM((NX, 2, 16, 128), F32),
            pltpu.VMEM((2, 2, 8, 128), F32),
            pltpu.VMEM((NC, 2, 8, 128), F32),
            pltpu.VMEM((NZ, 8, 128), F32),
            pltpu.VMEM((NC, 2, 8, 128), F32),
            pltpu.VMEM((NC, 2, 8, 128), F32),
            pltpu.VMEM((NX, 2, 16, 128), F32),
            pltpu.VMEM((NY, 16, 128), F32),
            pltpu.VMEM((NY, 16, 128), F32),
            pltpu.VMEM((NY, 16, 128), F32),
            pltpu.VMEM((2, 2, 16, 128), F32),
            pltpu.VMEM((NX, 2, 16, 128), F32),
            pltpu.VMEM((NX, 8, 128), F32),
            pltpu.VMEM((NX, 8, 128), F32),
            pltpu.VMEM((NC, 8, 128), F32),
            pltpu.VMEM((16, 256), F32),
            pltpu.VMEM((8, 128), F32),
            pltpu.VMEM((2, 16, 256), F32),
            pltpu.VMEM((TILES, 8, 128), F32),
            pltpu.SemaphoreType.DMA((9,)),
            pltpu.SemaphoreType.DMA((1,)),
            pltpu.SemaphoreType.DMA((STAGES,)),
        ],
        compiler_params=pltpu.CompilerParams(collective_id=0, has_side_effects=True),
    )(update_map, leaf_rhs, leaf_inverse, update_rows, sep_rhs, sep_inverse)
    leaf, sep = pl.pallas_call(
        finish,
        name="finish",
        out_shape=(jax.ShapeDtypeStruct((2, 16, 64), F32), jax.ShapeDtypeStruct((8, 16), F32)),
        in_specs=[vmem, vmem],
        out_specs=(vmem, vmem),
    )(pltpu.with_memory_space_constraint(leaf, pltpu.VMEM), pltpu.with_memory_space_constraint(sep, pltpu.VMEM))
    return leaf, sep.T


def solution(mesh):
    in_specs = (
        P("leaf", None, "col"),
        P("leaf", "row", "col"),
        P("leaf", "col", "row"),
        P("leaf", None),
        P(),
        P(("leaf", "row", "col"), None),
    )
    out_specs = (P("leaf", None, ("col", "row")), P(None, ("leaf", "row", "col")))
    return jax.shard_map(body, mesh=mesh, in_specs=in_specs, out_specs=out_specs, check_vma=False)
```
